32 devices in a mesh: wall: 4 (over y, core), surf: 8 (over z, x).
Axes of the slice: x: 2, y: 2, z: 4, core: 2. Of those that a mesh axis runs over, the one named last changes fastest.
Arguments:
- vector: bfloat16 [32, 16, 320, 256], P('surf', 'wall'), may hold values from -40 to 40
- lengths: int32 [32], P('surf'), may hold values from 1 to 16, as said below
- north_of: int32 [8, 4], P('surf'), may hold values from 0 to 3, each once within a row
- diagonal: bfloat16 [32, 16, 320, 320], P('surf', 'wall'), may hold values from -1 to 8
- lifting: bfloat16 [32, 16, 6, 80, 320], P('surf', 'wall'), may hold values from -0.625 to 0.625
- inverse_rows: bfloat16 [32, 16, 80, 320], P('surf', 'wall'), may hold values from -0.25 to 0.25
Outputs:
- next_basis: bfloat16 [32, 16, 320, 256], P('surf', 'wall')
- coefs: float32 [2, 256], replicated
The draws below stay inside these ranges and needn't reach their ends.
Inputs may be any that keep to these rules, and one draw needn't show every extreme that they name: `lengths`: in every patch of 4 lines one line has 16 elements and another has 1.
All inputs are finite; a program needn't handle non-finite values.
Results may differ from the reference program's by a relative error of at most 0.00135.
Values may be sent and summed in bfloat16 or wider, within the bound.
A program may use at most 64 MiB of HBM per device.

```python
import math
import jax
import jax.numpy as jnp
from jax import lax

VARS = 5
NODE1D = 4
BLOCK = 320
FACE = 80
LINES_DEV = 4
R = 256
PATCHES = 8
LINES = 32
WALLPOS = 16


def draw_vector(key, part):
    subkeys = jax.random.split(key, 2)
    line_frac = jnp.arange(LINES, dtype=jnp.float32) / max(LINES - 1, 1)
    jitter = jnp.exp(jax.random.uniform(subkeys[0], (LINES, WALLPOS), jnp.float32, 0.0, math.log(3.3)))
    element_scale = 3.0 ** (line_frac[:, None] - 0.5) * jitter / 1.8
    noise = jax.random.truncated_normal(subkeys[1], -6.0, 6.0, (LINES, WALLPOS, BLOCK, R), jnp.float32)
    return (noise * element_scale[:, :, None, None]).astype(jnp.bfloat16)


def draw_diagonal(key, part):
    subkeys = jax.random.split(key, 2)
    wall_frac = jnp.arange(WALLPOS, dtype=jnp.float32) / max(WALLPOS - 1, 1)
    line_frac = jnp.arange(LINES, dtype=jnp.float32) / max(LINES - 1, 1)
    jitter = jnp.exp(jax.random.uniform(subkeys[0], (LINES, WALLPOS), jnp.float32, 0.0, math.log(1.5)))
    shift_term = 0.25 * 5.0 ** wall_frac[None, :] * 2.0 ** line_frac[:, None] * jitter
    offdiag = jax.random.truncated_normal(subkeys[1], -6.0, 6.0, (LINES, WALLPOS, BLOCK, BLOCK), jnp.float32)
    offdiag = offdiag / math.sqrt(BLOCK)
    unit_matrix = jnp.eye(BLOCK, dtype=jnp.float32)
    return (offdiag + shift_term[:, :, None, None] * unit_matrix).astype(jnp.bfloat16)


def draw_lengths(key, part):
    subkeys = jax.random.split(key, 3)
    baseline = jax.random.randint(subkeys[0], (PATCHES, LINES_DEV), 1, WALLPOS + 1)
    longest = jax.random.randint(subkeys[1], (PATCHES, 1), 0, LINES_DEV)
    shortest = (longest + 1 + jax.random.randint(subkeys[2], (PATCHES, 1), 0, LINES_DEV - 1)) % LINES_DEV
    slots = jnp.arange(LINES_DEV)[None, :]
    baseline = jnp.where(slots == longest, WALLPOS, baseline)
    baseline = jnp.where(slots == shortest, 1, baseline)
    return baseline.reshape(LINES).astype(jnp.int32)


def steps_of(key, dims, shards, smallest, high):
    def one(axis_at, parts):
        draws = jax.random.uniform(jax.random.fold_in(jax.random.fold_in(key, 6), axis_at), (parts,), jnp.float32, smallest / len(shards), high / len(shards))
        return jnp.repeat(jnp.exp(draws), dims[axis_at] // parts).reshape((-1,) + (1,) * (len(dims) - axis_at - 1))

    gain = one(*shards[0])
    for cut in shards[1:]:
        gain = gain * one(*cut)
    return gain


def scatter_about(rng, dims, scale, reach, cuts=(), held_as=jnp.bfloat16):
    values = scale * jax.random.normal(rng, dims, jnp.float32)
    if cuts:
        values = values * steps_of(rng, dims, cuts, -0.22, 0.18)
    return jnp.clip(values, -reach, reach).astype(held_as)


def setup_inputs(seed: int = 0) -> dict:
    streams_of = jax.random.split(jax.random.key(seed), 7)
    vector = draw_vector(jax.random.fold_in(streams_of[6], 71), 0)
    lengths = draw_lengths(jax.random.fold_in(streams_of[6], 71), 0)
    north_of = jax.vmap(lambda own: jax.random.permutation(own, LINES_DEV))(jax.random.split(streams_of[2], PATCHES)).reshape((PATCHES, LINES_DEV)).astype(jnp.int32)
    diagonal = draw_diagonal(jax.random.fold_in(streams_of[6], 71), 0)
    lifting = scatter_about(streams_of[4], (LINES, WALLPOS, 6, FACE, BLOCK), FACE ** -0.5, 0.625, ((0, 8), (1, 4)))
    inverse_rows = scatter_about(streams_of[5], (LINES, WALLPOS, FACE, BLOCK), (2 * BLOCK) ** -0.5, 0.25, ((0, 8), (1, 4)))
    return {"vector": vector, "lengths": lengths, "north_of": north_of, "diagonal": diagonal, "lifting": lifting, "inverse_rows": inverse_rows}


FULL_ACCURACY = lax.Precision.HIGHEST

def face_traces(values):
    leading = values.shape[:-2]
    column_entries = values.shape[-1]
    nodal_cube = values.reshape(leading + (VARS, NODE1D, NODE1D, NODE1D, column_entries))
    last_node = NODE1D - 1

    def flatten(piece):
        return piece.reshape(leading + (FACE, column_entries))
    bottom_face = flatten(nodal_cube[..., 0, :])
    top_face = flatten(nodal_cube[..., last_node, :])
    west_face = flatten(nodal_cube[..., 0, :, :, :])
    east_face = flatten(nodal_cube[..., last_node, :, :, :])
    south_face = flatten(nodal_cube[..., 0, :, :])
    north_face = flatten(nodal_cube[..., last_node, :, :])
    return (bottom_face, top_face, west_face, east_face, south_face, north_face)

def reference(vector, lengths, north_of, diagonal, lifting, inverse_rows):
    positions = jnp.arange(WALLPOS, dtype=jnp.int32)
    living = (positions[None, :] < lengths[:, None]).astype(jnp.float32)
    masked = vector * living[:, :, None, None].astype(jnp.bfloat16)
    bottom_face, top_face, west_face, east_face, south_face, north_face = face_traces(masked)
    zero_row = jnp.zeros_like(top_face[:, :1])
    from_below = jnp.concatenate([zero_row, top_face[:, :-1]], axis=1)
    from_above = jnp.concatenate([bottom_face[:, 1:], zero_row], axis=1)
    from_west = jnp.roll(east_face, 1, axis=0)
    from_east = jnp.roll(west_face, -1, axis=0)
    patch_base = (jnp.arange(PATCHES, dtype=jnp.int32) * LINES_DEV)[:, None]
    north_line = (patch_base + north_of).reshape(LINES).astype(jnp.int32)
    south_line = jnp.zeros((LINES,), jnp.int32).at[north_line].set(jnp.arange(LINES, dtype=jnp.int32))
    from_north = south_face[north_line]
    from_south = north_face[south_line]
    neighbours = jnp.stack([from_below, from_above, from_west, from_east, from_south, from_north], axis=2)

    def per_line(pieces):
        diagonal_row_block, lifted_line_term, inverse_line, line_under_mask, adjacent_line, living_line = pieces
        matrix_product = jnp.einsum('ont,oti->oni', diagonal_row_block.astype(jnp.float32), line_under_mask.astype(jnp.float32), precision=FULL_ACCURACY)
        matrix_product = matrix_product + jnp.einsum('ovih,ovip->ohp', lifted_line_term.astype(jnp.float32), adjacent_line.astype(jnp.float32), precision=FULL_ACCURACY)
        matrix_product = matrix_product * living_line[:, None, None]

        def advance(carried, inputs):
            product_now, lower_lift, inverse_now, alive_now = inputs
            eliminated = alive_now * (product_now - jnp.dot(lower_lift.T, carried, precision=FULL_ACCURACY))
            return (jnp.dot(inverse_now, eliminated, precision=FULL_ACCURACY), eliminated)
        start = jnp.zeros((FACE, R), jnp.float32)
        _, eliminated = lax.scan(advance, start, (matrix_product, lifted_line_term[:, 0].astype(jnp.float32), inverse_line.astype(jnp.float32), living_line))
        return eliminated
    eliminated = lax.map(per_line, (diagonal, lifting, inverse_rows, masked, neighbours, living))
    masked_wide = masked.astype(jnp.float32)
    coupling_total = lax.optimization_barrier(jnp.sum(masked_wide * eliminated, axis=(0, 1, 2)))
    self_sum = lax.optimization_barrier(jnp.sum(masked_wide * masked_wide, axis=(0, 1, 2)))
    projection = coupling_total / self_sum
    remainder = eliminated - projection * masked_wide
    entries = LINES * WALLPOS * BLOCK
    spread = jnp.sqrt(lax.optimization_barrier(jnp.sum(remainder * remainder, axis=(0, 1, 2))) / entries + 1e-06)
    next_basis = (remainder / spread).astype(jnp.bfloat16)
    coefs = jnp.stack([projection, spread])
    return (next_basis, coefs)
```

```python
import functools

import jax
import jax.numpy as jnp
from jax import lax
from jax.experimental import pallas as pl
from jax.experimental.pallas import tpu as pltpu
from jax.sharding import PartitionSpec as P

NODE1D = 4
F32 = jnp.float32
BF16 = jnp.bfloat16
MESH = pl.DeviceIdType.MESH


def times(a, b):
    return lax.dot_general(a, b, (((1,), (0,)), ((), ())), preferred_element_type=F32)


def left_t(a, b):
    return lax.dot_general(a, b, (((0,), (0,)), ((), ())), preferred_element_type=F32)


def right_t(a, b):
    return lax.dot_general(a, b, (((1,), (1,)), ((), ())), preferred_element_type=F32)


def split(x):
    high = x.astype(BF16)
    return high, (x - high.astype(F32)).astype(BF16)


def selector(face, block):
    entry = lax.broadcasted_iota(jnp.int32, (face, block), 0)
    column = lax.broadcasted_iota(jnp.int32, (face, block), 1)
    last = NODE1D - 1
    along = NODE1D * entry
    across = NODE1D * NODE1D * (entry // NODE1D) + entry % NODE1D
    wanted = (along + last, along, across, across + last * NODE1D)
    return [jnp.where(column == at, 1.0, 0.0).astype(BF16) for at in wanted]


def merge(gathered, count):
    p = [gathered[i, 0:1] for i in range(count)]
    s = [gathered[i, 1:2] for i in range(count)]
    o = [gathered[i, 2:3] for i in range(count)]
    r = [gathered[i, 3:4] for i in range(count)]
    total = sum(s[1:], s[0])
    cross = sum((o[i] + p[i] * s[i] for i in range(1, count)), o[0] + p[0] * s[0])
    safe = jnp.where(total > 0.0, total, 1.0)
    common = jnp.where(total > 0.0, cross / safe, 0.0)
    odd = jnp.zeros_like(total)
    square = jnp.zeros_like(total)
    for i in range(count):
        shift = p[i] - common
        odd = odd + (o[i] + shift * s[i])
        square = square + (r[i] + shift * (2.0 * o[i] + shift * s[i]))
    return common, total, odd, square, cross


def kernel(
    sizes, lengths, north_of, vector, diagonal, lifting, inverse, basis, coefs,
    xv, dg, lf, iv, sel, top, bottom, west, east, south, north,
    below_in, above_in, west_in, east_in, prod, carry, carry_f, gt, q, mt, cin, cout,
    stat1, all1, stat2, all2,
    in_sem, halo_send, halo_recv, chain_send, chain_recv, s1_send, s1_recv, s2_send, s2_recv,
):
    lines, seg, block, face, cols, walls, surfs = sizes
    w = lax.axis_index("wall")
    s = lax.axis_index("surf")
    loads = []
    for n, (src, dst) in enumerate(((vector, xv), (diagonal, dg), (lifting, lf), (inverse, iv))):
        for l in range(lines):
            loads.append(pltpu.make_async_copy(src.at[l], dst.at[l], in_sem.at[n, l]))
    for copy in loads:
        copy.start()
    barrier = pltpu.get_barrier_semaphore()
    for d in range(1, walls):
        pl.semaphore_signal(
            barrier, inc=1, device_id={"wall": lax.rem(w + d, walls)}, device_id_type=MESH
        )
    for d in range(1, surfs):
        pl.semaphore_signal(
            barrier, inc=1, device_id={"surf": lax.rem(s + d, surfs)}, device_id_type=MESH
        )

    def alive(l, k):
        return jnp.where(w * seg + k < lengths[l], 1.0, 0.0).astype(F32)

    def element(i):
        return i // seg, i % seg

    for g, rows in enumerate(selector(face, block)):
        sel[g * face:(g + 1) * face] = rows
    plane = NODE1D * NODE1D
    cube = plane * NODE1D

    for copy in loads[:lines]:
        copy.wait()

    def mask_one(i, _):
        l, k = element(i)
        x = (xv[l, k].astype(F32) * alive(l, k)).astype(BF16)
        xv[l, k] = x
        west[l, k] = jnp.concatenate([x[v:v + plane] for v in range(0, block, cube)], axis=0)
        east[l + 1, k] = jnp.concatenate(
            [x[v + cube - plane:v + cube] for v in range(0, block, cube)], axis=0
        )
        return 0

    lax.fori_loop(0, lines * seg, mask_one, 0)
    pl.semaphore_wait(barrier, walls - 1 + surfs - 1)

    def remote(src, dst, send, recv, target):
        return pltpu.make_async_remote_copy(
            src_ref=src, dst_ref=dst, send_sem=send, recv_sem=recv,
            device_id=target, device_id_type=MESH,
        )

    to_east = remote(
        east.at[lines], west_in, halo_send.at[0], halo_recv.at[0],
        {"surf": lax.rem(s + 1, surfs)},
    )
    to_west = remote(
        west.at[0], east_in, halo_send.at[1], halo_recv.at[1],
        {"surf": lax.rem(s + surfs - 1, surfs)},
    )
    to_east.start()
    to_west.start()

    def trace_one(i, _):
        l, k = element(i)
        t = times(sel[...], xv[l, k]).astype(BF16)
        top[l, k + 1] = t[:face]
        bottom[l, k] = t[face:2 * face]
        south[l, k] = t[2 * face:3 * face]
        north[l, k] = t[3 * face:]
        return 0

    lax.fori_loop(0, lines * seg, trace_one, 0)

    up = {"wall": lax.rem(w + 1, walls)}
    down = {"wall": lax.rem(w + walls - 1, walls)}
    to_above = remote(top.at[:, seg], below_in, halo_send.at[2], halo_recv.at[2], up)
    to_below = remote(bottom.at[:, 0], above_in, halo_send.at[3], halo_recv.at[3], down)

    @pl.when(w < walls - 1)
    def _():
        to_above.start()

    @pl.when(w > 0)
    def _():
        to_below.start()

    for copy in loads[lines:]:
        copy.wait()

    def local_one(i, _):
        l, k = element(i)
        south_line = jnp.int32(0)
        for j in range(lines):
            south_line = jnp.where(north_of[0, j] == l, j, south_line)
        sides = jnp.concatenate([north[south_line, k], south[north_of[0, l], k]], axis=0)
        prod[l, k] = times(dg[l, k], xv[l, k]) + left_t(lf[l, k, 4 * face:6 * face], sides)
        return 0

    lax.fori_loop(0, lines * seg, local_one, 0)

    row = lax.broadcasted_iota(jnp.int32, (face, face), 0)
    column = lax.broadcasted_iota(jnp.int32, (face, face), 1)
    eye = jnp.where(row == column, 1.0, 0.0).astype(F32)
    for l in range(lines):
        q[l] = eye

    def map_step(k, _):
        for l in range(lines):
            qh, ql = split(q[l])
            lower = lf[l, k, 0:face]
            g = alive(l, k) * (times(qh, lower) + times(ql, lower))
            gh, gl = split(g)
            gt[l, k, 0:face] = gh
            gt[l, k, face:2 * face] = gl
            gt[l, k, 2 * face:3 * face] = gh
            q[l] = -(right_t(gh, iv[l, k]) + right_t(gl, iv[l, k]))
        return 0

    lax.fori_loop(0, seg, map_step, 0)
    for l in range(lines):
        mh, ml = split(q[l])
        mt[l, 0:face] = mh
        mt[l, face:2 * face] = ml
        mt[l, 2 * face:3 * face] = mh

    carry[...] = jnp.zeros_like(carry)

    @pl.when(w > 0)
    def _():
        to_above.wait_recv()
        for l in range(lines):
            top[l, 0] = below_in[l]

    @pl.when(w == 0)
    def _():
        for l in range(lines):
            top[l, 0] = jnp.zeros((face, cols), BF16)

    @pl.when(w < walls - 1)
    def _():
        to_below.wait_recv()
        for l in range(lines):
            bottom[l, seg] = above_in[l]

    @pl.when(w == walls - 1)
    def _():
        for l in range(lines):
            bottom[l, seg] = jnp.zeros((face, cols), BF16)

    to_east.wait_recv()
    east[0] = west_in[...]
    to_west.wait_recv()
    west[lines] = east_in[...]

    def free_step(k, _):
        for l in range(lines):
            blocks = jnp.concatenate(
                [lf[l, k, 0:4 * face], lf[l, k, 0:face], lf[l, k, 0:face]], axis=0
            )
            sides = jnp.concatenate(
                [top[l, k], bottom[l, k + 1], east[l, k], west[l + 1, k], carry[l]], axis=0
            )
            e = alive(l, k) * (prod[l, k] + left_t(blocks, sides))
            prod[l, k] = e
            eh, el = split(e)
            c = times(iv[l, k], eh) + times(iv[l, k], el)
            carry_f[l] = c
            ch, cl = split(-c)
            carry[l, 0:face] = ch
            carry[l, face:2 * face] = cl
        return 0

    lax.fori_loop(0, seg, free_step, 0)

    chain = [
        remote(cout.at[l], cin.at[l], chain_send.at[l], chain_recv.at[l], up)
        for l in range(lines)
    ]

    @pl.when(w == 0)
    def _():
        for l in range(lines):
            cout[l] = carry_f[l]
            chain[l].start()

    def first_sums(i, acc):
        l, k = element(i)
        x = xv[l, k].astype(F32)
        e = prod[l, k]
        xs = x.reshape(block // 8, 8, cols)
        es = e.reshape(block // 8, 8, cols)
        return acc[0] + jnp.sum(xs * es, axis=0), acc[1] + jnp.sum(xs * xs, axis=0)

    nothing = jnp.zeros((8, cols), F32)
    near, norm = lax.fori_loop(0, lines * seg, first_sums, (nothing, nothing))
    near = jnp.sum(near, axis=0, keepdims=True)
    norm = jnp.sum(norm, axis=0, keepdims=True)
    guess = jnp.where(norm > 0.0, near / jnp.where(norm > 0.0, norm, 1.0), 0.0)

    def packed(l):
        high, low = split(cin[l])
        return jnp.concatenate([high, high, low], axis=0)

    @pl.when(w > 0)
    def _():
        for l in range(lines):
            chain[l].wait_recv()

            @pl.when(w < walls - 1)
            def _():
                cout[l] = carry_f[l] + left_t(mt[l], packed(l))
                chain[l].start()

        def correct(i, _):
            l, k = element(i)
            prod[l, k] = prod[l, k] - left_t(gt[l, k], packed(l))
            return 0

        lax.fori_loop(0, lines * seg, correct, 0)

    def second_sums(i, acc):
        l, k = element(i)
        x = xv[l, k].astype(F32)
        e = prod[l, k] - guess * x
        xs = x.reshape(block // 8, 8, cols)
        es = e.reshape(block // 8, 8, cols)
        return acc[0] + jnp.sum(xs * es, axis=0), acc[1] + jnp.sum(es * es, axis=0)

    odd, square = lax.fori_loop(0, lines * seg, second_sums, (nothing, nothing))
    odd = jnp.sum(odd, axis=0, keepdims=True)
    square = jnp.sum(square, axis=0, keepdims=True)

    def gather(values, stat, slots, sends, recvs, axis, me, count):
        block_of = jnp.concatenate(list(values) + [jnp.zeros((4, cols), F32)], axis=0)
        stat[...] = block_of
        slots[me] = block_of
        copies = [
            remote(
                stat, slots.at[me], sends.at[d], recvs.at[d], {axis: lax.rem(me + d, count)}
            )
            for d in range(1, count)
        ]
        for copy in copies:
            copy.start()
        for copy in copies:
            copy.wait_recv()
        return copies

    sent1 = gather((guess, norm, odd, square), stat1, all1, s1_send, s1_recv, "wall", w, walls)
    common, total, odd, square, _ = merge(all1, walls)
    sent2 = gather((common, total, odd, square), stat2, all2, s2_send, s2_recv, "surf", s, surfs)
    _, total, _, square, cross = merge(all2, surfs)
    projection = cross / total
    entries = lines * seg * block * walls * surfs
    spread = jnp.sqrt(square / entries + 1e-06)
    coefs[0:1] = projection
    coefs[1:2] = spread
    scale = 1.0 / spread

    def finish(i, _):
        l, k = element(i)
        basis[l, k] = ((prod[l, k] - projection * xv[l, k].astype(F32)) * scale).astype(BF16)
        return 0

    lax.fori_loop(0, lines * seg, finish, 0)

    for copy in sent1 + sent2 + [to_east, to_west]:
        copy.wait_send()

    @pl.when(w < walls - 1)
    def _():
        to_above.wait_send()
        for copy in chain:
            copy.wait_send()

    @pl.when(w > 0)
    def _():
        to_below.wait_send()


def per_device(walls, surfs, vector, lengths, north_of, diagonal, lifting, inverse_rows):
    lines, seg, block, cols = vector.shape
    face = inverse_rows.shape[2]
    sizes = (lines, seg, block, face, cols, walls, surfs)
    stacked = lifting.reshape(lines, seg, lifting.shape[2] * face, block)
    smem = pl.BlockSpec(memory_space=pltpu.SMEM)
    vmem = pl.BlockSpec(memory_space=pltpu.VMEM)
    hbm = pl.BlockSpec(memory_space=pl.ANY)
    dma = pltpu.SemaphoreType.DMA
    return pl.pallas_call(
        functools.partial(kernel, sizes),
        out_shape=(
            jax.ShapeDtypeStruct(vector.shape, BF16),
            jax.ShapeDtypeStruct((2, cols), F32),
        ),
        in_specs=[smem, smem, hbm, hbm, hbm, hbm],
        out_specs=(vmem, vmem),
        scratch_shapes=[
            pltpu.VMEM(vector.shape, BF16),
            pltpu.VMEM(diagonal.shape, BF16),
            pltpu.VMEM(stacked.shape, BF16),
            pltpu.VMEM(inverse_rows.shape, BF16),
            pltpu.VMEM((4 * face, block), BF16),
            pltpu.VMEM((lines, seg + 1, face, cols), BF16),
            pltpu.VMEM((lines, seg + 1, face, cols), BF16),
            pltpu.VMEM((lines + 1, seg, face, cols), BF16),
            pltpu.VMEM((lines + 1, seg, face, cols), BF16),
            pltpu.VMEM((lines, seg, face, cols), BF16),
            pltpu.VMEM((lines, seg, face, cols), BF16),
            pltpu.VMEM((lines, face, cols), BF16),
            pltpu.VMEM((lines, face, cols), BF16),
            pltpu.VMEM((seg, face, cols), BF16),
            pltpu.VMEM((seg, face, cols), BF16),
            pltpu.VMEM(vector.shape, F32),
            pltpu.VMEM((lines, 2 * face, cols), BF16),
            pltpu.VMEM((lines, face, cols), F32),
            pltpu.VMEM((lines, seg, 3 * face, block), BF16),
            pltpu.VMEM((lines, face, face), F32),
            pltpu.VMEM((lines, 3 * face, face), BF16),
            pltpu.VMEM((lines, face, cols), F32),
            pltpu.VMEM((lines, face, cols), F32),
            pltpu.VMEM((8, cols), F32),
            pltpu.VMEM((walls, 8, cols), F32),
            pltpu.VMEM((8, cols), F32),
            pltpu.VMEM((surfs, 8, cols), F32),
            dma((4, lines)),
            dma((4,)),
            dma((4,)),
            dma((lines,)),
            dma((lines,)),
            dma((walls,)),
            dma((walls,)),
            dma((surfs,)),
            dma((surfs,)),
        ],
        compiler_params=pltpu.CompilerParams(
            collective_id=0, has_side_effects=True, vmem_limit_bytes=60 * 1024 * 1024
        ),
    )(lengths, north_of, vector, diagonal, stacked, inverse_rows)


def solution(mesh):
    in_specs = (
        P("surf", "wall", None, None),
        P("surf"),
        P("surf", None),
        P("surf", "wall", None, None),
        P("surf", "wall", None, None, None),
        P("surf", "wall", None, None),
    )
    out_specs = (P("surf", "wall", None, None), P())
    return jax.shard_map(
        functools.partial(per_device, mesh.shape["wall"], mesh.shape["surf"]),
        mesh=mesh, in_specs=in_specs, out_specs=out_specs, check_vma=False,
    )
```

```python
import functools

import jax
import jax.numpy as jnp
from jax import lax
from jax.experimental import pallas as pl
from jax.experimental.pallas import tpu as pltpu
from jax.sharding import PartitionSpec as P

NODE1D = 4
F32 = jnp.float32
BF16 = jnp.bfloat16
MESH = pl.DeviceIdType.MESH


def times(a, b):
    return lax.dot_general(a, b, (((1,), (0,)), ((), ())), preferred_element_type=F32)


def left_t(a, b):
    return lax.dot_general(a, b, (((0,), (0,)), ((), ())), preferred_element_type=F32)


def right_t(a, b):
    return lax.dot_general(a, b, (((1,), (1,)), ((), ())), preferred_element_type=F32)


def split(x):
    high = x.astype(BF16)
    return high, (x - high.astype(F32)).astype(BF16)


def selector(face, block):
    entry = lax.broadcasted_iota(jnp.int32, (face, block), 0)
    column = lax.broadcasted_iota(jnp.int32, (face, block), 1)
    last = NODE1D - 1
    along = NODE1D * entry
    across = NODE1D * NODE1D * (entry // NODE1D) + entry % NODE1D
    wanted = (along + last, along, across, across + last * NODE1D)
    return [jnp.where(column == at, 1.0, 0.0).astype(BF16) for at in wanted]


def merge(gathered, count):
    p = [gathered[i, 0:1] for i in range(count)]
    s = [gathered[i, 1:2] for i in range(count)]
    o = [gathered[i, 2:3] for i in range(count)]
    r = [gathered[i, 3:4] for i in range(count)]
    total = sum(s[1:], s[0])
    cross = sum((o[i] + p[i] * s[i] for i in range(1, count)), o[0] + p[0] * s[0])
    safe = jnp.where(total > 0.0, total, 1.0)
    common = jnp.where(total > 0.0, cross / safe, 0.0)
    odd = jnp.zeros_like(total)
    square = jnp.zeros_like(total)
    for i in range(count):
        shift = p[i] - common
        odd = odd + (o[i] + shift * s[i])
        square = square + (r[i] + shift * (2.0 * o[i] + shift * s[i]))
    return common, total, odd, square, cross


def kernel(
    sizes, lengths, north_of, vector, diagonal, lifting, inverse, xv, prod, coefs,
    dg, lf, iv, sel, top, bottom, west, east, south, north,
    below_in, above_in, west_in, east_in, carry, carry_f, gt, q, mt, cin, cpack, cout,
    stat1, all1, stat2, all2,
    in_sem, halo_send, halo_recv, chain_send, chain_recv, s1_send, s1_recv, s2_send, s2_recv,
):
    lines, seg, block, face, cols, walls, surfs = sizes
    w = lax.axis_index("wall")
    s = lax.axis_index("surf")
    loads = []
    for n, (src, dst) in enumerate(((vector, xv), (diagonal, dg), (lifting, lf), (inverse, iv))):
        for l in range(lines):
            loads.append(pltpu.make_async_copy(src.at[l], dst.at[l], in_sem.at[n, l]))
    for copy in loads:
        copy.start()
    barrier = pltpu.get_barrier_semaphore()
    for d in range(1, walls):
        pl.semaphore_signal(
            barrier, inc=1, device_id={"wall": lax.rem(w + d, walls)}, device_id_type=MESH
        )
    for d in range(1, surfs):
        pl.semaphore_signal(
            barrier, inc=1, device_id={"surf": lax.rem(s + d, surfs)}, device_id_type=MESH
        )

    def alive(l, k):
        return jnp.where(w * seg + k < lengths[l], 1.0, 0.0).astype(F32)

    def element(i):
        return i // seg, i % seg

    for g, rows in enumerate(selector(face, block)):
        sel[g * face:(g + 1) * face] = rows
    plane = NODE1D * NODE1D
    cube = plane * NODE1D

    for copy in loads[:lines]:
        copy.wait()

    def mask_one(i, _):
        l, k = element(i)
        x = (xv[l, k].astype(F32) * alive(l, k)).astype(BF16)
        xv[l, k] = x
        west[l, k] = jnp.concatenate([x[v:v + plane] for v in range(0, block, cube)], axis=0)
        east[l + 1, k] = jnp.concatenate(
            [x[v + cube - plane:v + cube] for v in range(0, block, cube)], axis=0
        )
        return 0

    lax.fori_loop(0, lines * seg, mask_one, 0)
    pl.semaphore_wait(barrier, walls - 1 + surfs - 1)

    def remote(src, dst, send, recv, target):
        return pltpu.make_async_remote_copy(
            src_ref=src, dst_ref=dst, send_sem=send, recv_sem=recv,
            device_id=target, device_id_type=MESH,
        )

    to_east = remote(
        east.at[lines], west_in, halo_send.at[0], halo_recv.at[0],
        {"surf": lax.rem(s + 1, surfs)},
    )
    to_west = remote(
        west.at[0], east_in, halo_send.at[1], halo_recv.at[1],
        {"surf": lax.rem(s + surfs - 1, surfs)},
    )
    to_east.start()
    to_west.start()

    def trace_one(i, _):
        l, k = element(i)
        t = times(sel[...], xv[l, k]).astype(BF16)
        top[l, k + 1] = t[:face]
        bottom[l, k] = t[face:2 * face]
        south[l, k] = t[2 * face:3 * face]
        north[l, k] = t[3 * face:]
        return 0

    lax.fori_loop(0, lines * seg, trace_one, 0, unroll=2)

    up = {"wall": lax.rem(w + 1, walls)}
    down = {"wall": lax.rem(w + walls - 1, walls)}
    to_above = remote(top.at[:, seg], below_in, halo_send.at[2], halo_recv.at[2], up)
    to_below = remote(bottom.at[:, 0], above_in, halo_send.at[3], halo_recv.at[3], down)

    @pl.when(w < walls - 1)
    def _():
        to_above.start()

    @pl.when(w > 0)
    def _():
        to_below.start()

    for copy in loads[lines:]:
        copy.wait()

    def local_one(i, _):
        l, k = element(i)
        south_line = jnp.int32(0)
        for j in range(lines):
            south_line = jnp.where(north_of[0, j] == l, j, south_line)
        sides = jnp.concatenate([north[south_line, k], south[north_of[0, l], k]], axis=0)
        prod[l, k] = times(dg[l, k], xv[l, k]) + left_t(lf[l, k, 4 * face:6 * face], sides)
        return 0

    lax.fori_loop(0, lines * seg, local_one, 0, unroll=2)

    row = lax.broadcasted_iota(jnp.int32, (face, face), 0)
    column = lax.broadcasted_iota(jnp.int32, (face, face), 1)
    eye = jnp.where(row == column, 1.0, 0.0).astype(F32)
    for l in range(lines):
        q[l] = eye

    def map_step(k, _):
        for l in range(lines):
            qh, ql = split(q[l])
            lower = lf[l, k, 0:face]
            g = alive(l, k) * (times(qh, lower) + times(ql, lower))
            gh, gl = split(g)
            gt[l, k, 0:face] = gh
            gt[l, k, face:2 * face] = gl
            gt[l, k, 2 * face:3 * face] = gh
            q[l] = -(right_t(gh, iv[l, k]) + right_t(gl, iv[l, k]))
        return 0

    lax.fori_loop(0, seg, map_step, 0)
    for l in range(lines):
        mh, ml = split(q[l])
        mt[l, 0:face] = mh
        mt[l, face:2 * face] = ml
        mt[l, 2 * face:3 * face] = mh

    carry[...] = jnp.zeros_like(carry)

    @pl.when(w > 0)
    def _():
        to_above.wait_recv()
        for l in range(lines):
            top[l, 0] = below_in[l]

    @pl.when(w == 0)
    def _():
        for l in range(lines):
            top[l, 0] = jnp.zeros((face, cols), BF16)

    @pl.when(w < walls - 1)
    def _():
        to_below.wait_recv()
        for l in range(lines):
            bottom[l, seg] = above_in[l]

    @pl.when(w == walls - 1)
    def _():
        for l in range(lines):
            bottom[l, seg] = jnp.zeros((face, cols), BF16)

    to_east.wait_recv()
    east[0] = west_in[...]
    to_west.wait_recv()
    west[lines] = east_in[...]

    def free_step(k, _):
        for l in range(lines):
            blocks = jnp.concatenate(
                [lf[l, k, 0:4 * face], lf[l, k, 0:face], lf[l, k, 0:face]], axis=0
            )
            sides = jnp.concatenate(
                [top[l, k], bottom[l, k + 1], east[l, k], west[l + 1, k], carry[l]], axis=0
            )
            e = alive(l, k) * (prod[l, k] + left_t(blocks, sides))
            prod[l, k] = e
            eh, el = split(e)
            c = times(iv[l, k], eh) + times(iv[l, k], el)
            carry_f[l] = c
            ch, cl = split(-c)
            carry[l, 0:face] = ch
            carry[l, face:2 * face] = cl
        return 0

    lax.fori_loop(0, seg, free_step, 0)

    chain = [
        remote(cout.at[l], cin.at[l], chain_send.at[l], chain_recv.at[l], up)
        for l in range(lines)
    ]

    @pl.when(w == 0)
    def _():
        for l in range(lines):
            cout[l] = carry_f[l]
            chain[l].start()

    def first_sums(i, acc):
        l, k = element(i)
        x = xv[l, k].astype(F32)
        e = prod[l, k]
        xs = x.reshape(block // 8, 8, cols)
        es = e.reshape(block // 8, 8, cols)
        return acc[0] + jnp.sum(xs * es, axis=0), acc[1] + jnp.sum(xs * xs, axis=0)

    nothing = jnp.zeros((8, cols), F32)
    near, norm = lax.fori_loop(0, lines * seg, first_sums, (nothing, nothing))
    near = jnp.sum(near, axis=0, keepdims=True)
    norm = jnp.sum(norm, axis=0, keepdims=True)
    guess = jnp.where(norm > 0.0, near / jnp.where(norm > 0.0, norm, 1.0), 0.0)

    @pl.when(w == 0)
    def _():
        cpack[...] = jnp.zeros_like(cpack)

    @pl.when(w > 0)
    def _():
        for l in range(lines):
            chain[l].wait_recv()
            high, low = split(cin[l])
            cpack[l] = jnp.concatenate([high, high, low], axis=0)

            @pl.when(w < walls - 1)
            def _():
                cout[l] = carry_f[l] + left_t(mt[l], cpack[l])
                chain[l].start()

    def correct(i, acc):
        l, k = element(i)
        e = prod[l, k] - left_t(gt[l, k], cpack[l])
        prod[l, k] = e
        x = xv[l, k].astype(F32)
        e = e - guess * x
        xs = x.reshape(block // 8, 8, cols)
        es = e.reshape(block // 8, 8, cols)
        return acc[0] + jnp.sum(xs * es, axis=0), acc[1] + jnp.sum(es * es, axis=0)

    odd, square = lax.fori_loop(0, lines * seg, correct, (nothing, nothing), unroll=2)
    odd = jnp.sum(odd, axis=0, keepdims=True)
    square = jnp.sum(square, axis=0, keepdims=True)

    def gather(values, stat, slots, sends, recvs, axis, me, count):
        block_of = jnp.concatenate(list(values) + [jnp.zeros((4, cols), F32)], axis=0)
        stat[...] = block_of
        slots[me] = block_of
        copies = [
            remote(
                stat, slots.at[me], sends.at[d], recvs.at[d], {axis: lax.rem(me + d, count)}
            )
            for d in range(1, count)
        ]
        for copy in copies:
            copy.start()
        for copy in copies:
            copy.wait_recv()
        return copies

    sent1 = gather((guess, norm, odd, square), stat1, all1, s1_send, s1_recv, "wall", w, walls)
    common, total, odd, square, _ = merge(all1, walls)
    sent2 = gather((common, total, odd, square), stat2, all2, s2_send, s2_recv, "surf", s, surfs)
    _, total, _, square, cross = merge(all2, surfs)
    projection = cross / total
    entries = lines * seg * block * walls * surfs
    spread = jnp.sqrt(square / entries + 1e-06)
    coefs[0:1] = projection
    coefs[1:2] = spread
    for copy in sent1 + sent2 + [to_east, to_west]:
        copy.wait_send()

    @pl.when(w < walls - 1)
    def _():
        to_above.wait_send()
        for copy in chain:
            copy.wait_send()

    @pl.when(w > 0)
    def _():
        to_below.wait_send()


def finish(masked, eliminated, stats, basis, coefs):
    l = pl.program_id(0)
    coefs[...] = stats[...]
    projection = stats[0:1]
    scale = 1.0 / stats[1:2]
    for k in range(basis.shape[1]):
        x = masked[l, k].astype(F32)
        basis[0, k] = ((eliminated[l, k] - projection * x) * scale).astype(BF16)


def per_device(walls, surfs, vector, lengths, north_of, diagonal, lifting, inverse_rows):
    lines, seg, block, cols = vector.shape
    face = inverse_rows.shape[2]
    sizes = (lines, seg, block, face, cols, walls, surfs)
    stacked = lifting.reshape(lines, seg, lifting.shape[2] * face, block)
    smem = pl.BlockSpec(memory_space=pltpu.SMEM)
    vmem = pl.BlockSpec(memory_space=pltpu.VMEM)
    hbm = pl.BlockSpec(memory_space=pltpu.HBM)
    dma = pltpu.SemaphoreType.DMA
    masked, eliminated, stats = pl.pallas_call(
        functools.partial(kernel, sizes),
        out_shape=(
            pltpu.VMEM(vector.shape, BF16),
            pltpu.VMEM(vector.shape, F32),
            pltpu.VMEM((2, cols), F32),
        ),
        in_specs=[smem, smem, hbm, hbm, hbm, hbm],
        out_specs=(vmem, vmem, vmem),
        scratch_shapes=[
            pltpu.VMEM(diagonal.shape, BF16),
            pltpu.VMEM(stacked.shape, BF16),
            pltpu.VMEM(inverse_rows.shape, BF16),
            pltpu.VMEM((4 * face, block), BF16),
            pltpu.VMEM((lines, seg + 1, face, cols), BF16),
            pltpu.VMEM((lines, seg + 1, face, cols), BF16),
            pltpu.VMEM((lines + 1, seg, face, cols), BF16),
            pltpu.VMEM((lines + 1, seg, face, cols), BF16),
            pltpu.VMEM((lines, seg, face, cols), BF16),
            pltpu.VMEM((lines, seg, face, cols), BF16),
            pltpu.VMEM((lines, face, cols), BF16),
            pltpu.VMEM((lines, face, cols), BF16),
            pltpu.VMEM((seg, face, cols), BF16),
            pltpu.VMEM((seg, face, cols), BF16),
            pltpu.VMEM((lines, 2 * face, cols), BF16),
            pltpu.VMEM((lines, face, cols), F32),
            pltpu.VMEM((lines, seg, 3 * face, block), BF16),
            pltpu.VMEM((lines, face, face), F32),
            pltpu.VMEM((lines, 3 * face, face), BF16),
            pltpu.VMEM((lines, face, cols), F32),
            pltpu.VMEM((lines, 3 * face, cols), BF16),
            pltpu.VMEM((lines, face, cols), F32),
            pltpu.VMEM((8, cols), F32),
            pltpu.VMEM((walls, 8, cols), F32),
            pltpu.VMEM((8, cols), F32),
            pltpu.VMEM((surfs, 8, cols), F32),
            dma((4, lines)),
            dma((4,)),
            dma((4,)),
            dma((lines,)),
            dma((lines,)),
            dma((walls,)),
            dma((walls,)),
            dma((surfs,)),
            dma((surfs,)),
        ],
        compiler_params=pltpu.CompilerParams(
            collective_id=0, has_side_effects=True, vmem_limit_bytes=56 * 1024 * 1024
        ),
    )(lengths, north_of, vector, diagonal, stacked, inverse_rows)
    return pl.pallas_call(
        finish,
        grid=(lines,),
        out_shape=(
            jax.ShapeDtypeStruct(vector.shape, BF16),
            jax.ShapeDtypeStruct((2, cols), F32),
        ),
        in_specs=[vmem, vmem, vmem],
        out_specs=(
            pl.BlockSpec((1, seg, block, cols), lambda l: (l, 0, 0, 0)),
            pl.BlockSpec((2, cols), lambda l: (0, 0)),
        ),
        compiler_params=pltpu.CompilerParams(vmem_limit_bytes=16 * 1024 * 1024),
    )(masked, eliminated, stats)


def solution(mesh):
    in_specs = (
        P("surf", "wall", None, None),
        P("surf"),
        P("surf", None),
        P("surf", "wall", None, None),
        P("surf", "wall", None, None, None),
        P("surf", "wall", None, None),
    )
    out_specs = (P("surf", "wall", None, None), P())
    return jax.shard_map(
        functools.partial(per_device, mesh.shape["wall"], mesh.shape["surf"]),
        mesh=mesh, in_specs=in_specs, out_specs=out_specs, check_vma=False,
    )
```

```python
import functools

import jax
import jax.numpy as jnp
from jax import lax
from jax.experimental import pallas as pl
from jax.experimental.pallas import tpu as pltpu
from jax.sharding import PartitionSpec as P

NODE1D = 4
F32 = jnp.float32
BF16 = jnp.bfloat16
MESH = pl.DeviceIdType.MESH


def times(a, b):
    return lax.dot_general(a, b, (((1,), (0,)), ((), ())), preferred_element_type=F32)


def left_t(a, b):
    return lax.dot_general(a, b, (((0,), (0,)), ((), ())), preferred_element_type=F32)


def right_t(a, b):
    return lax.dot_general(a, b, (((1,), (1,)), ((), ())), preferred_element_type=F32)


def split(x):
    high = x.astype(BF16)
    return high, (x - high.astype(F32)).astype(BF16)


def selector(face, block):
    entry = lax.broadcasted_iota(jnp.int32, (face, block), 0)
    column = lax.broadcasted_iota(jnp.int32, (face, block), 1)
    last = NODE1D - 1
    along = NODE1D * entry
    across = NODE1D * NODE1D * (entry // NODE1D) + entry % NODE1D
    wanted = (along + last, along, across, across + last * NODE1D)
    return [jnp.where(column == at, 1.0, 0.0).astype(BF16) for at in wanted]


def merge(gathered, count):
    p = [gathered[i, 0:1] for i in range(count)]
    s = [gathered[i, 1:2] for i in range(count)]
    o = [gathered[i, 2:3] for i in range(count)]
    r = [gathered[i, 3:4] for i in range(count)]
    total = sum(s[1:], s[0])
    cross = sum((o[i] + p[i] * s[i] for i in range(1, count)), o[0] + p[0] * s[0])
    safe = jnp.where(total > 0.0, total, 1.0)
    common = jnp.where(total > 0.0, cross / safe, 0.0)
    odd = jnp.zeros_like(total)
    square = jnp.zeros_like(total)
    for i in range(count):
        shift = p[i] - common
        odd = odd + (o[i] + shift * s[i])
        square = square + (r[i] + shift * (2.0 * o[i] + shift * s[i]))
    return common, total, odd, square, cross


def kernel(
    sizes, lengths, north_of, vector, diagonal, lifting, inverse, xv, prod, coefs,
    dg, lf, iv, sel, top, bottom, west, east, south, north,
    below_in, above_in, west_in, east_in, carry, carry_f, gt, q, mt, cin, cpack, cout,
    stat1, all1, stat2, all2,
    in_sem, halo_send, halo_recv, chain_send, chain_recv, s1_send, s1_recv, s2_send, s2_recv,
):
    lines, seg, block, face, cols, walls, surfs = sizes
    w = lax.axis_index("wall")
    s = lax.axis_index("surf")
    loads = []
    for n, (src, dst) in enumerate(((vector, xv), (diagonal, dg), (lifting, lf), (inverse, iv))):
        for l in range(lines):
            loads.append(pltpu.make_async_copy(src.at[l], dst.at[l], in_sem.at[n, l]))
    first = sorted(range(lines), key=lambda l: min(l, lines - 1 - l))
    for copy in [loads[l] for l in first] + loads[lines:]:
        copy.start()
    barrier = pltpu.get_barrier_semaphore()
    for d in range(1, walls):
        pl.semaphore_signal(
            barrier, inc=1, device_id={"wall": lax.rem(w + d, walls)}, device_id_type=MESH
        )
    for d in range(1, surfs):
        pl.semaphore_signal(
            barrier, inc=1, device_id={"surf": lax.rem(s + d, surfs)}, device_id_type=MESH
        )

    def alive(l, k):
        return jnp.where(w * seg + k < lengths[l], 1.0, 0.0).astype(F32)

    def element(i):
        return i // seg, i % seg

    for g, rows in enumerate(selector(face, block)):
        sel[g * face:(g + 1) * face] = rows
    plane = NODE1D * NODE1D
    cube = plane * NODE1D

    def mask_one(l, k):
        x = (xv[l, k].astype(F32) * alive(l, k)).astype(BF16)
        xv[l, k] = x
        west[l, k] = jnp.concatenate([x[v:v + plane] for v in range(0, block, cube)], axis=0)
        east[l + 1, k] = jnp.concatenate(
            [x[v + cube - plane:v + cube] for v in range(0, block, cube)], axis=0
        )

    def mask_line(l):
        def one(k, _):
            mask_one(l, k)
            return 0

        loads[l].wait()
        lax.fori_loop(0, seg, one, 0)

    outer = sorted({0, lines - 1})
    inner = [l for l in range(lines) if l not in outer]
    for l in outer:
        mask_line(l)
    pl.semaphore_wait(barrier, walls - 1 + surfs - 1)

    def remote(src, dst, send, recv, target):
        return pltpu.make_async_remote_copy(
            src_ref=src, dst_ref=dst, send_sem=send, recv_sem=recv,
            device_id=target, device_id_type=MESH,
        )

    to_east = remote(
        east.at[lines], west_in, halo_send.at[0], halo_recv.at[0],
        {"surf": lax.rem(s + 1, surfs)},
    )
    to_west = remote(
        west.at[0], east_in, halo_send.at[1], halo_recv.at[1],
        {"surf": lax.rem(s + surfs - 1, surfs)},
    )
    to_east.start()
    to_west.start()
    for l in inner:
        mask_line(l)

    def trace_one(i, _):
        l, k = element(i)
        t = times(sel[...], xv[l, k]).astype(BF16)
        top[l, k + 1] = t[:face]
        bottom[l, k] = t[face:2 * face]
        south[l, k] = t[2 * face:3 * face]
        north[l, k] = t[3 * face:]
        return 0

    lax.fori_loop(0, lines * seg, trace_one, 0, unroll=2)

    up = {"wall": lax.rem(w + 1, walls)}
    down = {"wall": lax.rem(w + walls - 1, walls)}
    to_above = remote(top.at[:, seg], below_in, halo_send.at[2], halo_recv.at[2], up)
    to_below = remote(bottom.at[:, 0], above_in, halo_send.at[3], halo_recv.at[3], down)

    @pl.when(w < walls - 1)
    def _():
        to_above.start()

    @pl.when(w > 0)
    def _():
        to_below.start()

    for copy in loads[lines:]:
        copy.wait()

    def local_one(i, _):
        l, k = element(i)
        south_line = jnp.int32(0)
        for j in range(lines):
            south_line = jnp.where(north_of[0, j] == l, j, south_line)
        sides = jnp.concatenate([north[south_line, k], south[north_of[0, l], k]], axis=0)
        prod[l, k] = times(dg[l, k], xv[l, k]) + left_t(lf[l, k, 4 * face:6 * face], sides)
        return 0

    lax.fori_loop(0, lines * seg, local_one, 0, unroll=2)

    row = lax.broadcasted_iota(jnp.int32, (face, face), 0)
    column = lax.broadcasted_iota(jnp.int32, (face, face), 1)
    eye = jnp.where(row == column, 1.0, 0.0).astype(F32)
    for l in range(lines):
        q[l] = eye

    def map_step(k, _):
        for l in range(lines):
            qh, ql = split(q[l])
            lower = lf[l, k, 0:face]
            g = alive(l, k) * (times(qh, lower) + times(ql, lower))
            gh, gl = split(g)
            gt[l, k, 0:face] = gh
            gt[l, k, face:2 * face] = gl
            gt[l, k, 2 * face:3 * face] = gh
            q[l] = -(right_t(gh, iv[l, k]) + right_t(gl, iv[l, k]))
        return 0

    lax.fori_loop(0, seg, map_step, 0)
    for l in range(lines):
        mh, ml = split(q[l])
        mt[l, 0:face] = mh
        mt[l, face:2 * face] = ml
        mt[l, 2 * face:3 * face] = mh

    carry[...] = jnp.zeros_like(carry)

    @pl.when(w > 0)
    def _():
        to_above.wait_recv()
        for l in range(lines):
            top[l, 0] = below_in[l]

    @pl.when(w == 0)
    def _():
        for l in range(lines):
            top[l, 0] = jnp.zeros((face, cols), BF16)

    @pl.when(w < walls - 1)
    def _():
        to_below.wait_recv()
        for l in range(lines):
            bottom[l, seg] = above_in[l]

    @pl.when(w == walls - 1)
    def _():
        for l in range(lines):
            bottom[l, seg] = jnp.zeros((face, cols), BF16)

    def free_step(group, k, _):
        for l in group:
            blocks = jnp.concatenate(
                [lf[l, k, 0:4 * face], lf[l, k, 0:face], lf[l, k, 0:face]], axis=0
            )
            sides = jnp.concatenate(
                [top[l, k], bottom[l, k + 1], east[l, k], west[l + 1, k], carry[l]], axis=0
            )
            e = alive(l, k) * (prod[l, k] + left_t(blocks, sides))
            prod[l, k] = e
            eh, el = split(e)
            c = times(iv[l, k], eh) + times(iv[l, k], el)
            carry_f[l] = c
            ch, cl = split(-c)
            carry[l, 0:face] = ch
            carry[l, face:2 * face] = cl
        return 0

    chain = [
        remote(cout.at[l], cin.at[l], chain_send.at[l], chain_recv.at[l], up)
        for l in range(lines)
    ]

    def begin(group):
        @pl.when(w == 0)
        def _():
            for l in group:
                cout[l] = carry_f[l]
                chain[l].start()

    def take(l):
        chain[l].wait_recv()
        high, low = split(cin[l])
        cpack[l] = jnp.concatenate([high, high, low], axis=0)

        @pl.when(w < walls - 1)
        def _():
            cout[l] = carry_f[l] + left_t(mt[l], cpack[l])
            chain[l].start()

    lax.fori_loop(0, seg, functools.partial(free_step, inner), 0)
    begin(inner)
    to_east.wait_recv()
    east[0] = west_in[...]
    to_west.wait_recv()
    west[lines] = east_in[...]
    part = 3 * seg // 4
    lax.fori_loop(0, part, functools.partial(free_step, outer), 0)

    @pl.when(w == 1)
    def _():
        for l in inner:
            take(l)

    lax.fori_loop(part, seg, functools.partial(free_step, outer), 0)
    begin(outer)

    def first_sums(i, acc):
        l, k = element(i)
        x = xv[l, k].astype(F32)
        e = prod[l, k]
        xs = x.reshape(block // 8, 8, cols)
        es = e.reshape(block // 8, 8, cols)
        return acc[0] + jnp.sum(xs * es, axis=0), acc[1] + jnp.sum(xs * xs, axis=0)

    nothing = jnp.zeros((8, cols), F32)
    near, norm = lax.fori_loop(0, lines * seg, first_sums, (nothing, nothing))
    near = jnp.sum(near, axis=0, keepdims=True)
    norm = jnp.sum(norm, axis=0, keepdims=True)
    guess = jnp.where(norm > 0.0, near / jnp.where(norm > 0.0, norm, 1.0), 0.0)

    @pl.when(w == 0)
    def _():
        cpack[...] = jnp.zeros_like(cpack)

    @pl.when(w > 1)
    def _():
        for l in inner:
            take(l)

    @pl.when(w > 0)
    def _():
        for l in outer:
            take(l)

    def correct(i, acc):
        l, k = element(i)
        e = prod[l, k] - left_t(gt[l, k], cpack[l])
        prod[l, k] = e
        x = xv[l, k].astype(F32)
        e = e - guess * x
        xs = x.reshape(block // 8, 8, cols)
        es = e.reshape(block // 8, 8, cols)
        return acc[0] + jnp.sum(xs * es, axis=0), acc[1] + jnp.sum(es * es, axis=0)

    odd, square = lax.fori_loop(0, lines * seg, correct, (nothing, nothing), unroll=2)
    odd = jnp.sum(odd, axis=0, keepdims=True)
    square = jnp.sum(square, axis=0, keepdims=True)

    def gather(values, stat, slots, sends, recvs, axis, me, count):
        block_of = jnp.concatenate(list(values) + [jnp.zeros((4, cols), F32)], axis=0)
        stat[...] = block_of
        slots[me] = block_of
        copies = [
            remote(
                stat, slots.at[me], sends.at[d], recvs.at[d], {axis: lax.rem(me + d, count)}
            )
            for d in range(1, count)
        ]
        for copy in copies:
            copy.start()
        for copy in copies:
            copy.wait_recv()
        return copies

    sent1 = gather((guess, norm, odd, square), stat1, all1, s1_send, s1_recv, "wall", w, walls)
    common, total, odd, square, _ = merge(all1, walls)
    sent2 = gather((common, total, odd, square), stat2, all2, s2_send, s2_recv, "surf", s, surfs)
    _, total, _, square, cross = merge(all2, surfs)
    projection = cross / total
    entries = lines * seg * block * walls * surfs
    spread = jnp.sqrt(square / entries + 1e-06)
    coefs[0:1] = projection
    coefs[1:2] = spread
    for copy in sent1 + sent2 + [to_east, to_west]:
        copy.wait_send()

    @pl.when(w < walls - 1)
    def _():
        to_above.wait_send()
        for copy in chain:
            copy.wait_send()

    @pl.when(w > 0)
    def _():
        to_below.wait_send()


def finish(masked, eliminated, stats, basis, coefs):
    l = pl.program_id(0)
    coefs[...] = stats[...]
    projection = stats[0:1]
    scale = 1.0 / stats[1:2]
    for k in range(basis.shape[1]):
        x = masked[l, k].astype(F32)
        basis[0, k] = ((eliminated[l, k] - projection * x) * scale).astype(BF16)


def per_device(walls, surfs, vector, lengths, north_of, diagonal, lifting, inverse_rows):
    lines, seg, block, cols = vector.shape
    face = inverse_rows.shape[2]
    sizes = (lines, seg, block, face, cols, walls, surfs)
    stacked = lifting.reshape(lines, seg, lifting.shape[2] * face, block)
    smem = pl.BlockSpec(memory_space=pltpu.SMEM)
    vmem = pl.BlockSpec(memory_space=pltpu.VMEM)
    hbm = pl.BlockSpec(memory_space=pltpu.HBM)
    dma = pltpu.SemaphoreType.DMA
    masked, eliminated, stats = pl.pallas_call(
        functools.partial(kernel, sizes),
        out_shape=(
            pltpu.VMEM(vector.shape, BF16),
            pltpu.VMEM(vector.shape, F32),
            pltpu.VMEM((2, cols), F32),
        ),
        in_specs=[smem, smem, hbm, hbm, hbm, hbm],
        out_specs=(vmem, vmem, vmem),
        scratch_shapes=[
            pltpu.VMEM(diagonal.shape, BF16),
            pltpu.VMEM(stacked.shape, BF16),
            pltpu.VMEM(inverse_rows.shape, BF16),
            pltpu.VMEM((4 * face, block), BF16),
            pltpu.VMEM((lines, seg + 1, face, cols), BF16),
            pltpu.VMEM((lines, seg + 1, face, cols), BF16),
            pltpu.VMEM((lines + 1, seg, face, cols), BF16),
            pltpu.VMEM((lines + 1, seg, face, cols), BF16),
            pltpu.VMEM((lines, seg, face, cols), BF16),
            pltpu.VMEM((lines, seg, face, cols), BF16),
            pltpu.VMEM((lines, face, cols), BF16),
            pltpu.VMEM((lines, face, cols), BF16),
            pltpu.VMEM((seg, face, cols), BF16),
            pltpu.VMEM((seg, face, cols), BF16),
            pltpu.VMEM((lines, 2 * face, cols), BF16),
            pltpu.VMEM((lines, face, cols), F32),
            pltpu.VMEM((lines, seg, 3 * face, block), BF16),
            pltpu.VMEM((lines, face, face), F32),
            pltpu.VMEM((lines, 3 * face, face), BF16),
            pltpu.VMEM((lines, face, cols), F32),
            pltpu.VMEM((lines, 3 * face, cols), BF16),
            pltpu.VMEM((lines, face, cols), F32),
            pltpu.VMEM((8, cols), F32),
            pltpu.VMEM((walls, 8, cols), F32),
            pltpu.VMEM((8, cols), F32),
            pltpu.VMEM((surfs, 8, cols), F32),
            dma((4, lines)),
            dma((4,)),
            dma((4,)),
            dma((lines,)),
            dma((lines,)),
            dma((walls,)),
            dma((walls,)),
            dma((surfs,)),
            dma((surfs,)),
        ],
        compiler_params=pltpu.CompilerParams(
            collective_id=0, has_side_effects=True, vmem_limit_bytes=56 * 1024 * 1024
        ),
    )(lengths, north_of, vector, diagonal, stacked, inverse_rows)
    return pl.pallas_call(
        finish,
        grid=(lines,),
        out_shape=(
            jax.ShapeDtypeStruct(vector.shape, BF16),
            jax.ShapeDtypeStruct((2, cols), F32),
        ),
        in_specs=[vmem, vmem, vmem],
        out_specs=(
            pl.BlockSpec((1, seg, block, cols), lambda l: (l, 0, 0, 0)),
            pl.BlockSpec((2, cols), lambda l: (0, 0)),
        ),
        compiler_params=pltpu.CompilerParams(vmem_limit_bytes=16 * 1024 * 1024),
    )(masked, eliminated, stats)


def solution(mesh):
    in_specs = (
        P("surf", "wall", None, None),
        P("surf"),
        P("surf", None),
        P("surf", "wall", None, None),
        P("surf", "wall", None, None, None),
        P("surf", "wall", None, None),
    )
    out_specs = (P("surf", "wall", None, None), P())
    return jax.shard_map(
        functools.partial(per_device, mesh.shape["wall"], mesh.shape["surf"]),
        mesh=mesh, in_specs=in_specs, out_specs=out_specs, check_vma=False,
    )
```
